512 devices in a mesh: freq: 8 (over z_hi, core), depth: 64 (over z_lo, y, x).
Axes of the slice: x: 4, y: 8, z: 8 (z_hi: 4, z_lo: 2; z = z_hi * 2 + z_lo), core: 2. Of those that a mesh axis runs over, the one named last changes fastest.
Arguments:
- green_source: bfloat16 [16, 64, 384, 2, 256], P('freq', 'depth'), may hold values from -6 to 6
- green_receiver: bfloat16 [16, 64, 128, 2, 256], P('freq', 'depth'), may hold values from -6 to 6
- source_index: int32 [1024], replicated, may hold values from 0 to 383
- receiver_index: int32 [1024], replicated, may hold values from 0 to 127
- frequency_bins: int32 [16], P('freq'), may hold values from 0 to 127
- depth_profile: float32 [64], P('depth'), may hold values from 0.5 to 2
Outputs:
- kernels: float32 [4, 1024, 64], P(None, ('freq', 'depth'))
The draws below stay inside these ranges and needn't reach their ends.
All inputs are finite; a program needn't handle non-finite values.
Results may differ from the reference program's by a relative error of at most 0.0015.
Values may be sent and summed in bfloat16 or wider, within the bound.
A program may use at most 64 MiB of HBM per device.

```python
import math
import jax
import jax.numpy as jnp
from jax import lax

NBINS = 128
W = 16
Z = 64
HS = 384
HR = 128
WX = 16
WY = 16
NP = 1024


def place_ends(drawn, own_key, smallest, high):
    longest = drawn.shape.index(max(drawn.shape))
    spots = []
    for shift in (0, 1):
        where = [jax.random.randint(jax.random.fold_in(own_key, axis), (), 0, length) for axis, length in enumerate(drawn.shape)]
        where[longest] = (where[longest] + shift) % drawn.shape[longest]
        spots.append(tuple(where))
    return drawn.at[spots[0]].set(smallest).at[spots[1]].set(high)


def block_levels(rng, dims, split, least, top_value):
    factor_of = 1.0
    for axis_at, shards_of in split:
        heights = jax.random.uniform(jax.random.fold_in(jax.random.fold_in(rng, 6), axis_at), (shards_of,), jnp.float32, least / len(split), top_value / len(split))
        factor_of = factor_of * jnp.repeat(jnp.exp(heights), dims[axis_at] // shards_of).reshape((-1,) + (1,) * (len(dims) - 1 - axis_at))
    return factor_of


def normal_values(stream_key, shape, deviation, limit, pieces=(), held_as=jnp.bfloat16):
    values = jax.random.normal(stream_key, shape, jnp.float32) * deviation
    if len(pieces) > 0:
        values = block_levels(stream_key, shape, pieces, -0.22, 0.18) * values
    return jnp.clip(values, min=-limit, max=limit).astype(held_as)


def setup_inputs(seed: int = 0) -> dict:
    streams_of = jax.random.split(jax.random.key(seed), 7)
    green_source = normal_values(streams_of[0], (W, Z, HS, 2, WX * WY), 1.0, 6.0, ((0, 8), (1, 64)))
    green_receiver = normal_values(streams_of[1], (W, Z, HR, 2, WX * WY), 1.0, 6.0, ((0, 8), (1, 64)))
    source_index = place_ends(jax.random.randint(streams_of[2], (NP,), 0, HS), jax.random.fold_in(streams_of[2], 1), 0, HS - 1).astype(jnp.int32)
    receiver_index = place_ends(jax.random.randint(streams_of[3], (NP,), 0, HR), jax.random.fold_in(streams_of[3], 1), 0, HR - 1).astype(jnp.int32)
    frequency_bins = place_ends(jax.random.randint(streams_of[4], (W,), 0, NBINS), jax.random.fold_in(streams_of[4], 1), 0, NBINS - 1).astype(jnp.int32)
    depth_profile = jnp.clip(jnp.exp(math.log(2.0) - 1.3862944 * jax.random.uniform(streams_of[5], (Z,), jnp.float32) ** block_levels(streams_of[5], (Z,), ((0, 64),), -0.2, 0.2)), 0.5, 2.0)
    return {"green_source": green_source, "green_receiver": green_receiver, "source_index": source_index, "receiver_index": receiver_index, "frequency_bins": frequency_bins, "depth_profile": depth_profile}


def window_slope(values, direction):
    window = values.reshape(values.shape[:-1] + (WX, WY))
    axis_index = window.ndim - 2 + direction
    extent = window.shape[axis_index]
    widths = [(0, 0)] * axis_index + [(1, 1)] + [(0, 0)] * (window.ndim - axis_index - 1)
    padded = jnp.pad(window, widths)
    upper = lax.slice_in_dim(padded, 2, extent + 2, axis=axis_index)
    lower = lax.slice_in_dim(padded, 0, extent, axis=axis_index)
    return (0.5 * (upper - lower)).reshape(values.shape)

def source_rows(current, layer_above, layer_below):
    real_part = current[..., 0, :]
    imag_part = current[..., 1, :]
    real_wide = real_part.astype(jnp.float32)
    imag_wide = imag_part.astype(jnp.float32)
    slope_real_x = window_slope(real_wide, 0).astype(jnp.bfloat16)
    slope_imag_x = window_slope(imag_wide, 0).astype(jnp.bfloat16)
    slope_real_y = window_slope(real_wide, 1).astype(jnp.bfloat16)
    slope_imag_y = window_slope(imag_wide, 1).astype(jnp.bfloat16)
    blocks = [jnp.concatenate([real_part, -imag_part], axis=-1), jnp.concatenate([slope_imag_x, slope_real_x], axis=-1), jnp.concatenate([slope_imag_y, slope_real_y], axis=-1), jnp.concatenate([layer_above[..., 1, :], layer_above[..., 0, :]], axis=-1), jnp.concatenate([layer_below[..., 1, :], layer_below[..., 0, :]], axis=-1)]
    return jnp.stack(blocks, axis=-3)

def reference(green_source, green_receiver, source_index, receiver_index, frequency_bins, depth_profile):
    scaled_freq = 0.5 + frequency_bins.astype(jnp.float32) / NBINS
    kernel_scale = 1.0 / math.sqrt(2.0 * WX * WY * W)

    def depth_layer(level):
        current = lax.dynamic_index_in_dim(green_source, level, axis=1, keepdims=False)
        upper_level = jnp.minimum(level + 1, Z - 1).astype(jnp.int32)
        lower_level = jnp.maximum(level - 1, 0).astype(jnp.int32)
        layer_above = lax.dynamic_index_in_dim(green_source, upper_level, axis=1, keepdims=False)
        layer_below = lax.dynamic_index_in_dim(green_source, lower_level, axis=1, keepdims=False)
        layer_above = jnp.where(level + 1 < Z, layer_above, jnp.zeros_like(layer_above))
        layer_below = jnp.where(level >= 1, layer_below, jnp.zeros_like(layer_below))
        left_rows = source_rows(current, layer_above, layer_below)
        left_pairs = left_rows[:, :, source_index].astype(jnp.float32)
        receiver_rows = lax.dynamic_index_in_dim(green_receiver, level, axis=1, keepdims=False)
        receiver_rows = receiver_rows.reshape(W, HR, 2 * WX * WY)
        right_pairs = receiver_rows[:, receiver_index].astype(jnp.float32)
        picked = jnp.einsum('wkpm,wpm->wkp', left_pairs, right_pairs)
        coupling = lax.dynamic_index_in_dim(depth_profile, level, axis=0, keepdims=False)
        first = picked[:, 0] * (scaled_freq * scaled_freq)[:, None] * coupling
        second = picked[:, 1] * scaled_freq[:, None]
        third = picked[:, 2] * scaled_freq[:, None]
        fourth = 0.5 * (picked[:, 3] - picked[:, 4]) * scaled_freq[:, None]
        stacked = jnp.stack([first, second, third, fourth], axis=1)
        return lax.optimization_barrier(jnp.sum(stacked, axis=0)) * kernel_scale
    layers = lax.map(depth_layer, jnp.arange(Z, dtype=jnp.int32))
    return jnp.transpose(layers, (1, 2, 0))
```

```python
import functools
import math

import jax
import jax.numpy as jnp
from jax import lax
from jax.experimental import pallas as pl
from jax.experimental.pallas import tpu as pltpu
from jax.sharding import PartitionSpec as P

NBINS = 128
WX = 16
WY = 16
CELLS = WX * WY
ZL = 2
LANES = 128
CHANNELS = 8
MESH = pl.DeviceIdType.MESH


def contract_cells(left, right):
    return lax.dot_general(
        left, right, (((1,), (1,)), ((), ())), preferred_element_type=jnp.float32
    )


def split_parts(value):
    high = value.astype(jnp.bfloat16)
    low = (value - high.astype(jnp.float32)).astype(jnp.bfloat16)
    return high, low


def adjoint_slopes(block):
    wide = block.astype(jnp.float32)
    cell = lax.broadcasted_iota(jnp.int32, wide.shape, 1)
    column = lax.rem(cell, WY)
    before_x = jnp.where(cell >= WY, pltpu.roll(wide, WY, 1), 0.0)
    after_x = jnp.where(cell < CELLS - WY, pltpu.roll(wide, CELLS - WY, 1), 0.0)
    before_y = jnp.where(column >= 1, pltpu.roll(wide, 1, 1), 0.0)
    after_y = jnp.where(column < WY - 1, pltpu.roll(wide, CELLS - 1, 1), 0.0)
    return split_parts(0.5 * (before_x - after_x)) + split_parts(0.5 * (before_y - after_y))


def kernel(
    n_freq, n_depth, scale,
    src, rec, sidx, ridx, bins, profile, out,
    near, onehot, terms, sbuf1, rbuf1, square1, sbuf2, rbuf2, square2,
    near_send, near_recv, send1, recv1, send2, recv2,
):
    f = lax.axis_index("freq")
    d = lax.axis_index("depth")
    group = n_freq * ZL
    plane = n_depth // ZL
    zl = d // plane
    q = d % plane
    g = f * ZL + zl
    slots, _, receivers, _ = rec.shape
    sources = src.shape[2]
    pairs = sidx.shape[1]
    part = pairs // group
    chunk = min(256, pairs)
    above = (d + 1) % n_depth
    below = (d + n_depth - 1) % n_depth

    barrier = pltpu.get_barrier_semaphore()

    def column_device(member):
        return (member // ZL, (member % ZL) * plane + q)

    def plane_device(member):
        return (f, zl * plane + member)

    for target in (above, below):
        pl.semaphore_signal(barrier, inc=1, device_id=(f, target), device_id_type=MESH)

    @pl.loop(1, group)
    def _(step):
        pl.semaphore_signal(
            barrier, inc=1, device_id=column_device((g + step) % group), device_id_type=MESH
        )

    @pl.loop(1, plane)
    def _(step):
        pl.semaphore_signal(
            barrier, inc=1, device_id=plane_device((q + step) % plane), device_id_type=MESH
        )

    pl.semaphore_wait(barrier, 2 + group - 1 + plane - 1)

    near_copies = []
    for slot in range(slots):
        for side, target in enumerate((above, below)):
            copy = pltpu.make_async_remote_copy(
                src_ref=rec.at[slot],
                dst_ref=near.at[side, slot],
                send_sem=near_send.at[side, slot],
                recv_sem=near_recv.at[side, slot],
                device_id=(f, target),
                device_id_type=MESH,
            )
            copy.start()
            near_copies.append(copy)

    source_rows = lax.broadcasted_iota(jnp.int32, (sources, pairs), 0)
    onehot[...] = jnp.where(source_rows == sidx[...], 1.0, 0.0).astype(jnp.bfloat16)
    terms[...] = jnp.zeros_like(terms)
    square1[...] = jnp.zeros_like(square1)
    square2[...] = jnp.zeros_like(square2)

    def pick(full, first):
        high, low = split_parts(full)
        count = full.shape[0] // receivers
        for start in range(0, pairs, chunk):
            hot = onehot[:, start : start + chunk]
            rows = jnp.dot(high, hot, preferred_element_type=jnp.float32) + jnp.dot(
                low, hot, preferred_element_type=jnp.float32
            )
            wanted = (
                lax.broadcasted_iota(jnp.int32, (receivers, chunk), 0)
                == ridx[:, start : start + chunk]
            )
            for channel in range(count):
                block = rows[channel * receivers : (channel + 1) * receivers]
                terms[first + channel : first + channel + 1, start : start + chunk] = jnp.sum(
                    jnp.where(wanted, block, 0.0), axis=0, keepdims=True
                )

    weights = [0.5 + bins[slot].astype(jnp.float32) * (1.0 / NBINS) for slot in range(slots)]
    own = None
    for slot in range(slots):
        r_re = rec[slot, 0]
        r_im = rec[slot, 1]
        left_re = jnp.concatenate((r_re,) + adjoint_slopes(r_im), axis=0)
        left_im = jnp.concatenate((-r_im,) + adjoint_slopes(r_re), axis=0)
        full = contract_cells(left_re, src[slot, 0]) + contract_cells(left_im, src[slot, 1])
        parts = [full[i * receivers : (i + 1) * receivers] for i in range(5)]
        weight = weights[slot]
        first = parts[0] * (weight * weight * profile[0] * scale)
        second = (parts[1] + parts[2]) * (weight * scale)
        third = (parts[3] + parts[4]) * (weight * scale)
        fresh = jnp.concatenate([first, second, third], axis=0)
        own = fresh if own is None else own + fresh
    pick(own, 0)

    beside = None
    for slot in range(slots):
        for side in range(2):
            near_copies[slot * 2 + side].wait_recv()
        left_re = jnp.concatenate([near[0, slot, 1], near[1, slot, 1]], axis=0)
        left_im = jnp.concatenate([near[0, slot, 0], near[1, slot, 0]], axis=0)
        full = contract_cells(left_re, src[slot, 0]) + contract_cells(left_im, src[slot, 1])
        fresh = full * (0.5 * weights[slot] * scale)
        beside = fresh if beside is None else beside + fresh
    pick(beside, 3)

    for member in range(group):
        sbuf1[member, :, 0:part] = terms[:, member * part : (member + 1) * part]

    def copy1(step):
        member = (g + step) % group
        return pltpu.make_async_remote_copy(
            src_ref=sbuf1.at[member],
            dst_ref=rbuf1.at[g],
            send_sem=send1.at[member],
            recv_sem=recv1.at[g],
            device_id=column_device(member),
            device_id_type=MESH,
        )

    def arrived1(step):
        member = (g + step) % group
        return pltpu.make_async_remote_copy(
            src_ref=sbuf1.at[member],
            dst_ref=rbuf1.at[member],
            send_sem=send1.at[member],
            recv_sem=recv1.at[member],
            device_id=column_device(member),
            device_id_type=MESH,
        )

    @pl.loop(1, group)
    def _(step):
        copy1(step).start()

    rbuf1[g] = sbuf1[g]

    @pl.loop(1, group)
    def _(step):
        arrived1(step).wait_recv()

    for low in range(ZL):
        total = rbuf1[low, :, 0:part]
        for member in range(1, n_freq):
            total = total + rbuf1[member * ZL + low, :, 0:part]
        square1[low * CHANNELS : (low + 1) * CHANNELS, 0:part] = total
    turned = square1[...].T
    for member in range(plane):
        sbuf2[member] = turned[2 * member : 2 * member + 2]

    def copy2(step):
        member = (q + step) % plane
        return pltpu.make_async_remote_copy(
            src_ref=sbuf2.at[member],
            dst_ref=rbuf2.at[q],
            send_sem=send2.at[member],
            recv_sem=recv2.at[q],
            device_id=plane_device(member),
            device_id_type=MESH,
        )

    def arrived2(step):
        member = (q + step) % plane
        return pltpu.make_async_remote_copy(
            src_ref=sbuf2.at[member],
            dst_ref=rbuf2.at[member],
            send_sem=send2.at[member],
            recv_sem=recv2.at[member],
            device_id=plane_device(member),
            device_id_type=MESH,
        )

    @pl.loop(1, plane)
    def _(step):
        copy2(step).start()

    rbuf2[q] = sbuf2[q]

    @pl.loop(1, plane)
    def _(step):
        arrived2(step).wait_recv()

    for owned in range(2):
        square2[owned * plane : (owned + 1) * plane, :] = rbuf2[:, owned, :]
    columns = square2[...].T
    gap = jnp.zeros((1, 1), jnp.float32)
    for owned in range(2):
        spread = slice(owned * plane, (owned + 1) * plane)
        depths = jnp.concatenate(
            [columns[low * CHANNELS : (low + 1) * CHANNELS, spread] for low in range(ZL)], axis=1
        )
        for channel in range(3):
            out[channel, owned : owned + 1, :] = depths[channel : channel + 1]
        upper = jnp.concatenate([depths[3:4, 1:], gap], axis=1)
        lower = jnp.concatenate([gap, depths[4:5, :-1]], axis=1)
        out[3, owned : owned + 1, :] = upper - lower

    for copy in near_copies:
        copy.wait_send()

    @pl.loop(1, group)
    def _(step):
        copy1(step).wait_send()

    @pl.loop(1, plane)
    def _(step):
        copy2(step).wait_send()


def on_device(
    green_source, green_receiver, source_index, receiver_index, frequency_bins, depth_profile
):
    slots, _, sources, _, cells = green_source.shape
    receivers = green_receiver.shape[2]
    pairs = source_index.shape[0]
    n_freq = lax.axis_size("freq")
    n_depth = lax.axis_size("depth")
    group = n_freq * ZL
    plane = n_depth // ZL
    scale = 1.0 / math.sqrt(2.0 * WX * WY * slots * n_freq)
    src = jnp.transpose(green_source[:, 0], (0, 2, 1, 3))
    rec = jnp.transpose(green_receiver[:, 0], (0, 2, 1, 3))
    vmem = pl.BlockSpec(memory_space=pltpu.VMEM)
    smem = pl.BlockSpec(memory_space=pltpu.SMEM)
    return pl.pallas_call(
        functools.partial(kernel, n_freq, n_depth, scale),
        out_shape=jax.ShapeDtypeStruct((4, pairs // (n_freq * n_depth), n_depth), jnp.float32),
        in_specs=[vmem, vmem, vmem, vmem, smem, smem],
        out_specs=vmem,
        scratch_shapes=[
            pltpu.VMEM((2, slots, 2, receivers, cells), jnp.bfloat16),
            pltpu.VMEM((sources, pairs), jnp.bfloat16),
            pltpu.VMEM((CHANNELS, pairs), jnp.float32),
            pltpu.VMEM((group, CHANNELS, LANES), jnp.float32),
            pltpu.VMEM((group, CHANNELS, LANES), jnp.float32),
            pltpu.VMEM((LANES, LANES), jnp.float32),
            pltpu.VMEM((plane, 2, LANES), jnp.float32),
            pltpu.VMEM((plane, 2, LANES), jnp.float32),
            pltpu.VMEM((LANES, LANES), jnp.float32),
            pltpu.SemaphoreType.DMA((2, slots)),
            pltpu.SemaphoreType.DMA((2, slots)),
            pltpu.SemaphoreType.DMA((group,)),
            pltpu.SemaphoreType.DMA((group,)),
            pltpu.SemaphoreType.DMA((plane,)),
            pltpu.SemaphoreType.DMA((plane,)),
        ],
        compiler_params=pltpu.CompilerParams(collective_id=0, has_side_effects=True),
    )(
        src,
        rec,
        source_index.reshape(1, pairs),
        receiver_index.reshape(1, pairs),
        frequency_bins,
        depth_profile,
    )


def solution(mesh):
    placed = (
        P("freq", "depth", None, None, None),
        P("freq", "depth", None, None, None),
        P(),
        P(),
        P("freq"),
        P("depth"),
    )
    return jax.shard_map(
        on_device,
        mesh=mesh,
        in_specs=placed,
        out_specs=P(None, ("freq", "depth"), None),
        check_vma=False,
    )
```

```python
import functools
import math

import jax
import jax.numpy as jnp
from jax import lax
from jax.experimental import pallas as pl
from jax.experimental.pallas import tpu as pltpu
from jax.sharding import PartitionSpec as P

NBINS = 128
WX = 16
WY = 16
CELLS = WX * WY
ZL = 2
LANES = 128
CHANNELS = 8
MESH = pl.DeviceIdType.MESH


def contract_cells(left, right):
    return lax.dot_general(
        left, right, (((1,), (1,)), ((), ())), preferred_element_type=jnp.float32
    )


def split_parts(value):
    high = value.astype(jnp.bfloat16)
    low = (value - high.astype(jnp.float32)).astype(jnp.bfloat16)
    return high, low


def adjoint_slopes(block):
    wide = block.astype(jnp.float32)
    cell = lax.broadcasted_iota(jnp.int32, wide.shape, 1)
    column = lax.rem(cell, WY)
    before_x = jnp.where(cell >= WY, pltpu.roll(wide, WY, 1), 0.0)
    after_x = jnp.where(cell < CELLS - WY, pltpu.roll(wide, CELLS - WY, 1), 0.0)
    before_y = jnp.where(column >= 1, pltpu.roll(wide, 1, 1), 0.0)
    after_y = jnp.where(column < WY - 1, pltpu.roll(wide, CELLS - 1, 1), 0.0)
    return split_parts(0.5 * (before_x - after_x)) + split_parts(0.5 * (before_y - after_y))


def kernel(
    n_freq, n_depth, scale,
    source, receiver, sidx, ridx, bins, profile, out,
    src_raw, rec_raw, src, rec, near, onehot, terms, sbuf1, rbuf1, square1, sbuf2, rbuf2, square2,
    fetch, near_send, near_recv, send1, recv1, send2, recv2,
):
    f = lax.axis_index("freq")
    d = lax.axis_index("depth")
    group = n_freq * ZL
    plane = n_depth // ZL
    zl = d // plane
    q = d % plane
    g = f * ZL + zl
    slots, _, receivers, _ = rec.shape
    sources = src.shape[2]
    pairs = sidx.shape[1]
    part = pairs // group
    chunk = min(256, pairs)
    above = (d + 1) % n_depth
    below = (d + n_depth - 1) % n_depth

    fetch_rec = pltpu.make_async_copy(receiver, rec_raw, fetch.at[0])
    fetch_src = pltpu.make_async_copy(source, src_raw, fetch.at[1])
    fetch_rec.start()
    fetch_src.start()
    barrier = pltpu.get_barrier_semaphore()

    def column_device(member):
        return (member // ZL, (member % ZL) * plane + q)

    def plane_device(member):
        return (f, zl * plane + member)

    for target in (above, below):
        pl.semaphore_signal(barrier, inc=1, device_id=(f, target), device_id_type=MESH)

    @pl.loop(1, group)
    def _(step):
        pl.semaphore_signal(
            barrier, inc=1, device_id=column_device((g + step) % group), device_id_type=MESH
        )

    @pl.loop(1, plane)
    def _(step):
        pl.semaphore_signal(
            barrier, inc=1, device_id=plane_device((q + step) % plane), device_id_type=MESH
        )

    fetch_rec.wait()
    for slot in range(slots):
        for side in range(2):
            rec[slot, side] = rec_raw[slot, 0, :, side, :]
    fetch_src.wait()
    for slot in range(slots):
        for side in range(2):
            src[slot, side] = src_raw[slot, 0, :, side, :]
    source_rows = lax.broadcasted_iota(jnp.int32, (sources, pairs), 0)
    onehot[...] = jnp.where(source_rows == sidx[...], 1.0, 0.0).astype(jnp.bfloat16)
    terms[...] = jnp.zeros_like(terms)
    square1[...] = jnp.zeros_like(square1)
    square2[...] = jnp.zeros_like(square2)
    pl.semaphore_wait(barrier, 2 + group - 1 + plane - 1)

    near_copies = []
    for slot in range(slots):
        for side, target in enumerate((above, below)):
            copy = pltpu.make_async_remote_copy(
                src_ref=rec.at[slot],
                dst_ref=near.at[side, slot],
                send_sem=near_send.at[side, slot],
                recv_sem=near_recv.at[side, slot],
                device_id=(f, target),
                device_id_type=MESH,
            )
            copy.start()
            near_copies.append(copy)

    def pick(full, first):
        high, low = split_parts(full)
        count = full.shape[0] // receivers
        for start in range(0, pairs, chunk):
            hot = onehot[:, start : start + chunk]
            rows = jnp.dot(high, hot, preferred_element_type=jnp.float32) + jnp.dot(
                low, hot, preferred_element_type=jnp.float32
            )
            wanted = (
                lax.broadcasted_iota(jnp.int32, (receivers, chunk), 0)
                == ridx[:, start : start + chunk]
            )
            for channel in range(count):
                block = rows[channel * receivers : (channel + 1) * receivers]
                terms[first + channel : first + channel + 1, start : start + chunk] = jnp.sum(
                    jnp.where(wanted, block, 0.0), axis=0, keepdims=True
                )

    weights = [0.5 + bins[slot].astype(jnp.float32) * (1.0 / NBINS) for slot in range(slots)]
    own = None
    for slot in range(slots):
        r_re = rec[slot, 0]
        r_im = rec[slot, 1]
        left_re = jnp.concatenate((r_re,) + adjoint_slopes(r_im), axis=0)
        left_im = jnp.concatenate((-r_im,) + adjoint_slopes(r_re), axis=0)
        full = contract_cells(left_re, src[slot, 0]) + contract_cells(left_im, src[slot, 1])
        parts = [full[i * receivers : (i + 1) * receivers] for i in range(5)]
        weight = weights[slot]
        first = parts[0] * (weight * weight * profile[0] * scale)
        second = (parts[1] + parts[2]) * (weight * scale)
        third = (parts[3] + parts[4]) * (weight * scale)
        fresh = jnp.concatenate([first, second, third], axis=0)
        own = fresh if own is None else own + fresh
    pick(own, 0)

    beside = None
    for slot in range(slots):
        for side in range(2):
            near_copies[slot * 2 + side].wait_recv()
        left_re = jnp.concatenate([near[0, slot, 1], near[1, slot, 1]], axis=0)
        left_im = jnp.concatenate([near[0, slot, 0], near[1, slot, 0]], axis=0)
        full = contract_cells(left_re, src[slot, 0]) + contract_cells(left_im, src[slot, 1])
        fresh = full * (0.5 * weights[slot] * scale)
        beside = fresh if beside is None else beside + fresh
    pick(beside, 3)

    for member in range(group):
        pair_slice = slice(member * part, (member + 1) * part)
        for channel in range(5):
            row, lane = channel // 2, (channel % 2) * part
            sbuf1[member, row : row + 1, lane : lane + part] = terms[
                channel : channel + 1, pair_slice
            ]

    def copy1(step):
        member = (g + step) % group
        return pltpu.make_async_remote_copy(
            src_ref=sbuf1.at[member],
            dst_ref=rbuf1.at[g],
            send_sem=send1.at[member],
            recv_sem=recv1.at[g],
            device_id=column_device(member),
            device_id_type=MESH,
        )

    def arrived1(step):
        member = (g + step) % group
        return pltpu.make_async_remote_copy(
            src_ref=sbuf1.at[member],
            dst_ref=rbuf1.at[member],
            send_sem=send1.at[member],
            recv_sem=recv1.at[member],
            device_id=column_device(member),
            device_id_type=MESH,
        )

    @pl.loop(1, group)
    def _(step):
        copy1(step).start()

    rbuf1[g] = sbuf1[g]

    @pl.loop(1, group)
    def _(step):
        arrived1(step).wait_recv()

    for low in range(ZL):
        total = rbuf1[low]
        for member in range(1, n_freq):
            total = total + rbuf1[member * ZL + low]
        for channel in range(5):
            row, lane = channel // 2, (channel % 2) * part
            target = low * CHANNELS + channel
            square1[target : target + 1, 0:part] = total[row : row + 1, lane : lane + part]
    turned = square1[...].T
    for member in range(plane):
        sbuf2[member] = turned[2 * member : 2 * member + 2]

    def copy2(step):
        member = (q + step) % plane
        return pltpu.make_async_remote_copy(
            src_ref=sbuf2.at[member],
            dst_ref=rbuf2.at[q],
            send_sem=send2.at[member],
            recv_sem=recv2.at[q],
            device_id=plane_device(member),
            device_id_type=MESH,
        )

    def arrived2(step):
        member = (q + step) % plane
        return pltpu.make_async_remote_copy(
            src_ref=sbuf2.at[member],
            dst_ref=rbuf2.at[member],
            send_sem=send2.at[member],
            recv_sem=recv2.at[member],
            device_id=plane_device(member),
            device_id_type=MESH,
        )

    @pl.loop(1, plane)
    def _(step):
        copy2(step).start()

    rbuf2[q] = sbuf2[q]

    @pl.loop(1, plane)
    def _(step):
        arrived2(step).wait_recv()

    for owned in range(2):
        square2[owned * plane : (owned + 1) * plane, :] = rbuf2[:, owned, :]
    columns = square2[...].T
    gap = jnp.zeros((1, 1), jnp.float32)
    for owned in range(2):
        spread = slice(owned * plane, (owned + 1) * plane)
        depths = jnp.concatenate(
            [columns[low * CHANNELS : (low + 1) * CHANNELS, spread] for low in range(ZL)], axis=1
        )
        for channel in range(3):
            out[channel, owned : owned + 1, :] = depths[channel : channel + 1]
        upper = jnp.concatenate([depths[3:4, 1:], gap], axis=1)
        lower = jnp.concatenate([gap, depths[4:5, :-1]], axis=1)
        out[3, owned : owned + 1, :] = upper - lower

    for copy in near_copies:
        copy.wait_send()

    @pl.loop(1, group)
    def _(step):
        copy1(step).wait_send()

    @pl.loop(1, plane)
    def _(step):
        copy2(step).wait_send()


def on_device(
    green_source, green_receiver, source_index, receiver_index, frequency_bins, depth_profile
):
    slots, _, sources, _, cells = green_source.shape
    receivers = green_receiver.shape[2]
    pairs = source_index.shape[0]
    n_freq = lax.axis_size("freq")
    n_depth = lax.axis_size("depth")
    group = n_freq * ZL
    plane = n_depth // ZL
    scale = 1.0 / math.sqrt(2.0 * WX * WY * slots * n_freq)
    vmem = pl.BlockSpec(memory_space=pltpu.VMEM)
    anywhere = pl.BlockSpec(memory_space=pl.ANY)
    smem = pl.BlockSpec(memory_space=pltpu.SMEM)
    return pl.pallas_call(
        functools.partial(kernel, n_freq, n_depth, scale),
        out_shape=jax.ShapeDtypeStruct((4, pairs // (n_freq * n_depth), n_depth), jnp.float32),
        in_specs=[anywhere, anywhere, vmem, vmem, smem, smem],
        out_specs=vmem,
        scratch_shapes=[
            pltpu.VMEM(green_source.shape, jnp.bfloat16),
            pltpu.VMEM(green_receiver.shape, jnp.bfloat16),
            pltpu.VMEM((slots, 2, sources, cells), jnp.bfloat16),
            pltpu.VMEM((slots, 2, receivers, cells), jnp.bfloat16),
            pltpu.VMEM((2, slots, 2, receivers, cells), jnp.bfloat16),
            pltpu.VMEM((sources, pairs), jnp.bfloat16),
            pltpu.VMEM((CHANNELS, pairs), jnp.float32),
            pltpu.VMEM((group, 4, LANES), jnp.float32),
            pltpu.VMEM((group, 4, LANES), jnp.float32),
            pltpu.VMEM((LANES, LANES), jnp.float32),
            pltpu.VMEM((plane, 2, LANES), jnp.float32),
            pltpu.VMEM((plane, 2, LANES), jnp.float32),
            pltpu.VMEM((LANES, LANES), jnp.float32),
            pltpu.SemaphoreType.DMA((2,)),
            pltpu.SemaphoreType.DMA((2, slots)),
            pltpu.SemaphoreType.DMA((2, slots)),
            pltpu.SemaphoreType.DMA((group,)),
            pltpu.SemaphoreType.DMA((group,)),
            pltpu.SemaphoreType.DMA((plane,)),
            pltpu.SemaphoreType.DMA((plane,)),
        ],
        compiler_params=pltpu.CompilerParams(collective_id=0, has_side_effects=True),
    )(
        green_source,
        green_receiver,
        source_index.reshape(1, pairs),
        receiver_index.reshape(1, pairs),
        frequency_bins,
        depth_profile,
    )


def solution(mesh):
    placed = (
        P("freq", "depth", None, None, None),
        P("freq", "depth", None, None, None),
        P(),
        P(),
        P("freq"),
        P("depth"),
    )
    return jax.shard_map(
        on_device,
        mesh=mesh,
        in_specs=placed,
        out_specs=P(None, ("freq", "depth"), None),
        check_vma=False,
    )
```

```python
import functools
import math

import jax
import jax.numpy as jnp
from jax import lax
from jax.experimental import pallas as pl
from jax.experimental.pallas import tpu as pltpu
from jax.sharding import PartitionSpec as P

NBINS = 128
WX = 16
WY = 16
CELLS = WX * WY
ZL = 2
LANES = 128
CHANNELS = 8
MESH = pl.DeviceIdType.MESH


def contract_cells(left, right):
    return lax.dot_general(
        left, right, (((1,), (1,)), ((), ())), preferred_element_type=jnp.float32
    )


def split_parts(value):
    high = value.astype(jnp.bfloat16)
    low = (value - high.astype(jnp.float32)).astype(jnp.bfloat16)
    return high, low


def adjoint_slopes(block):
    wide = block.astype(jnp.float32)
    cell = lax.broadcasted_iota(jnp.int32, wide.shape, 1)
    column = lax.rem(cell, WY)
    before_x = jnp.where(cell >= WY, pltpu.roll(wide, WY, 1), 0.0)
    after_x = jnp.where(cell < CELLS - WY, pltpu.roll(wide, CELLS - WY, 1), 0.0)
    before_y = jnp.where(column >= 1, pltpu.roll(wide, 1, 1), 0.0)
    after_y = jnp.where(column < WY - 1, pltpu.roll(wide, CELLS - 1, 1), 0.0)
    return split_parts(0.5 * (before_x - after_x)) + split_parts(0.5 * (before_y - after_y))


def kernel(
    n_freq, n_depth, scale,
    source, receiver, sidx, ridx, bins, profile, out,
    src_raw, rec_raw, src, rec, near, onehot, terms, sbuf1, rbuf1, square1, sbuf2, rbuf2, square2,
    fetch, near_send, near_recv, send1, recv1, send2, recv2,
):
    f = lax.axis_index("freq")
    d = lax.axis_index("depth")
    group = n_freq * ZL
    plane = n_depth // ZL
    zl = d // plane
    q = d % plane
    g = f * ZL + zl
    slots, _, receivers, _ = rec.shape
    sources = src.shape[2]
    pairs = sidx.shape[1]
    part = pairs // group
    chunk = min(256, pairs)
    above = (d + 1) % n_depth
    below = (d + n_depth - 1) % n_depth

    fetch_rec = pltpu.make_async_copy(receiver, rec_raw, fetch.at[0])
    fetch_src = pltpu.make_async_copy(source, src_raw, fetch.at[1])
    fetch_rec.start()
    fetch_src.start()
    barrier = pltpu.get_barrier_semaphore()

    def column_device(member):
        return (member // ZL, (member % ZL) * plane + q)

    def plane_device(member):
        return (f, zl * plane + member)

    for target in (above, below):
        pl.semaphore_signal(barrier, inc=1, device_id=(f, target), device_id_type=MESH)

    @pl.loop(1, group)
    def _(step):
        pl.semaphore_signal(
            barrier, inc=1, device_id=column_device((g + step) % group), device_id_type=MESH
        )

    @pl.loop(1, plane)
    def _(step):
        pl.semaphore_signal(
            barrier, inc=1, device_id=plane_device((q + step) % plane), device_id_type=MESH
        )

    fetch_rec.wait()
    for slot in range(slots):
        for side in range(2):
            rec[slot, side] = rec_raw[slot, 0, :, side, :]
    fetch_src.wait()
    for slot in range(slots):
        for side in range(2):
            src[slot, side] = src_raw[slot, 0, :, side, :]
    source_rows = lax.broadcasted_iota(jnp.int32, (sources, pairs), 0)
    onehot[...] = jnp.where(source_rows == sidx[...], 1.0, 0.0).astype(jnp.bfloat16)
    terms[...] = jnp.zeros_like(terms)
    square1[...] = jnp.zeros_like(square1)
    square2[...] = jnp.zeros_like(square2)
    pl.semaphore_wait(barrier, 2 + group - 1 + plane - 1)

    near_copies = []
    for slot in range(slots):
        for half in range(2):
            for side, target in enumerate((above, below)):
                copy = pltpu.make_async_remote_copy(
                    src_ref=rec.at[slot, half],
                    dst_ref=near.at[side, slot, half],
                    send_sem=near_send.at[side, slot, half],
                    recv_sem=near_recv.at[side, slot, half],
                    device_id=(f, target),
                    device_id_type=MESH,
                )
                copy.start()
                near_copies.append(copy)

    def pick(full, first):
        high, low = split_parts(full)
        count = full.shape[0] // receivers
        for start in range(0, pairs, chunk):
            hot = onehot[:, start : start + chunk]
            rows = jnp.dot(high, hot, preferred_element_type=jnp.float32) + jnp.dot(
                low, hot, preferred_element_type=jnp.float32
            )
            wanted = (
                lax.broadcasted_iota(jnp.int32, (receivers, chunk), 0)
                == ridx[:, start : start + chunk]
            )
            for channel in range(count):
                block = rows[channel * receivers : (channel + 1) * receivers]
                terms[first + channel : first + channel + 1, start : start + chunk] = jnp.sum(
                    jnp.where(wanted, block, 0.0), axis=0, keepdims=True
                )

    weights = [0.5 + bins[slot].astype(jnp.float32) * (1.0 / NBINS) for slot in range(slots)]
    own = None
    for slot in range(slots):
        r_re = rec[slot, 0]
        r_im = rec[slot, 1]
        left_re = jnp.concatenate((r_re,) + adjoint_slopes(r_im), axis=0)
        left_im = jnp.concatenate((-r_im,) + adjoint_slopes(r_re), axis=0)
        full = contract_cells(left_re, src[slot, 0]) + contract_cells(left_im, src[slot, 1])
        parts = [full[i * receivers : (i + 1) * receivers] for i in range(5)]
        weight = weights[slot]
        first = parts[0] * (weight * weight * profile[0] * scale)
        second = (parts[1] + parts[2]) * (weight * scale)
        third = (parts[3] + parts[4]) * (weight * scale)
        fresh = jnp.concatenate([first, second, third], axis=0)
        own = fresh if own is None else own + fresh
    pick(own, 0)

    beside = None
    for slot in range(slots):
        for index in range(slot * 4, slot * 4 + 4):
            near_copies[index].wait_recv()
        left_re = jnp.concatenate([near[0, slot, 1], near[1, slot, 1]], axis=0)
        left_im = jnp.concatenate([near[0, slot, 0], near[1, slot, 0]], axis=0)
        full = contract_cells(left_re, src[slot, 0]) + contract_cells(left_im, src[slot, 1])
        fresh = full * (0.5 * weights[slot] * scale)
        beside = fresh if beside is None else beside + fresh
    pick(beside, 3)

    for member in range(group):
        pair_slice = slice(member * part, (member + 1) * part)
        for channel in range(5):
            row, lane = channel // 2, (channel % 2) * part
            sbuf1[member, row : row + 1, lane : lane + part] = terms[
                channel : channel + 1, pair_slice
            ]

    def copy1(step):
        member = (g + step) % group
        return pltpu.make_async_remote_copy(
            src_ref=sbuf1.at[member],
            dst_ref=rbuf1.at[g],
            send_sem=send1.at[member],
            recv_sem=recv1.at[g],
            device_id=column_device(member),
            device_id_type=MESH,
        )

    def arrived1(step):
        member = (g + step) % group
        return pltpu.make_async_remote_copy(
            src_ref=sbuf1.at[member],
            dst_ref=rbuf1.at[member],
            send_sem=send1.at[member],
            recv_sem=recv1.at[member],
            device_id=column_device(member),
            device_id_type=MESH,
        )

    @pl.loop(1, group)
    def _(step):
        copy1(step).start()

    rbuf1[g] = sbuf1[g]

    @pl.loop(1, group)
    def _(step):
        arrived1(step).wait_recv()

    for low in range(ZL):
        total = rbuf1[low]
        for member in range(1, n_freq):
            total = total + rbuf1[member * ZL + low]
        for channel in range(5):
            row, lane = channel // 2, (channel % 2) * part
            target = low * CHANNELS + channel
            square1[target : target + 1, 0:part] = total[row : row + 1, lane : lane + part]
    turned = square1[...].T
    for member in range(plane):
        sbuf2[member] = turned[2 * member : 2 * member + 2]

    def copy2(step):
        member = (q + step) % plane
        return pltpu.make_async_remote_copy(
            src_ref=sbuf2.at[member],
            dst_ref=rbuf2.at[q],
            send_sem=send2.at[member],
            recv_sem=recv2.at[q],
            device_id=plane_device(member),
            device_id_type=MESH,
        )

    def arrived2(step):
        member = (q + step) % plane
        return pltpu.make_async_remote_copy(
            src_ref=sbuf2.at[member],
            dst_ref=rbuf2.at[member],
            send_sem=send2.at[member],
            recv_sem=recv2.at[member],
            device_id=plane_device(member),
            device_id_type=MESH,
        )

    @pl.loop(1, plane)
    def _(step):
        copy2(step).start()

    rbuf2[q] = sbuf2[q]

    @pl.loop(1, plane)
    def _(step):
        arrived2(step).wait_recv()

    for owned in range(2):
        square2[owned * plane : (owned + 1) * plane, :] = rbuf2[:, owned, :]
    columns = square2[...].T
    gap = jnp.zeros((1, 1), jnp.float32)
    for owned in range(2):
        spread = slice(owned * plane, (owned + 1) * plane)
        depths = jnp.concatenate(
            [columns[low * CHANNELS : (low + 1) * CHANNELS, spread] for low in range(ZL)], axis=1
        )
        for channel in range(3):
            out[channel, owned : owned + 1, :] = depths[channel : channel + 1]
        upper = jnp.concatenate([depths[3:4, 1:], gap], axis=1)
        lower = jnp.concatenate([gap, depths[4:5, :-1]], axis=1)
        out[3, owned : owned + 1, :] = upper - lower

    for copy in near_copies:
        copy.wait_send()

    @pl.loop(1, group)
    def _(step):
        copy1(step).wait_send()

    @pl.loop(1, plane)
    def _(step):
        copy2(step).wait_send()


def on_device(
    green_source, green_receiver, source_index, receiver_index, frequency_bins, depth_profile
):
    slots, _, sources, _, cells = green_source.shape
    receivers = green_receiver.shape[2]
    pairs = source_index.shape[0]
    n_freq = lax.axis_size("freq")
    n_depth = lax.axis_size("depth")
    group = n_freq * ZL
    plane = n_depth // ZL
    scale = 1.0 / math.sqrt(2.0 * WX * WY * slots * n_freq)
    vmem = pl.BlockSpec(memory_space=pltpu.VMEM)
    anywhere = pl.BlockSpec(memory_space=pl.ANY)
    smem = pl.BlockSpec(memory_space=pltpu.SMEM)
    return pl.pallas_call(
        functools.partial(kernel, n_freq, n_depth, scale),
        out_shape=jax.ShapeDtypeStruct((4, pairs // (n_freq * n_depth), n_depth), jnp.float32),
        in_specs=[anywhere, anywhere, vmem, vmem, smem, smem],
        out_specs=vmem,
        scratch_shapes=[
            pltpu.VMEM(green_source.shape, jnp.bfloat16),
            pltpu.VMEM(green_receiver.shape, jnp.bfloat16),
            pltpu.VMEM((slots, 2, sources, cells), jnp.bfloat16),
            pltpu.VMEM((slots, 2, receivers, cells), jnp.bfloat16),
            pltpu.VMEM((2, slots, 2, receivers, cells), jnp.bfloat16),
            pltpu.VMEM((sources, pairs), jnp.bfloat16),
            pltpu.VMEM((CHANNELS, pairs), jnp.float32),
            pltpu.VMEM((group, 4, LANES), jnp.float32),
            pltpu.VMEM((group, 4, LANES), jnp.float32),
            pltpu.VMEM((LANES, LANES), jnp.float32),
            pltpu.VMEM((plane, 2, LANES), jnp.float32),
            pltpu.VMEM((plane, 2, LANES), jnp.float32),
            pltpu.VMEM((LANES, LANES), jnp.float32),
            pltpu.SemaphoreType.DMA((2,)),
            pltpu.SemaphoreType.DMA((2, slots, 2)),
            pltpu.SemaphoreType.DMA((2, slots, 2)),
            pltpu.SemaphoreType.DMA((group,)),
            pltpu.SemaphoreType.DMA((group,)),
            pltpu.SemaphoreType.DMA((plane,)),
            pltpu.SemaphoreType.DMA((plane,)),
        ],
        compiler_params=pltpu.CompilerParams(collective_id=0, has_side_effects=True),
    )(
        green_source,
        green_receiver,
        source_index.reshape(1, pairs),
        receiver_index.reshape(1, pairs),
        frequency_bins,
        depth_profile,
    )


def solution(mesh):
    placed = (
        P("freq", "depth", None, None, None),
        P("freq", "depth", None, None, None),
        P(),
        P(),
        P("freq"),
        P("depth"),
    )
    return jax.shard_map(
        on_device,
        mesh=mesh,
        in_specs=placed,
        out_specs=P(None, ("freq", "depth"), None),
        check_vma=False,
    )
```
